32 devices in a mesh: groups: 2 (over y), rows: 4 (over x, core), seq: 4 (over z).
Axes of the slice: x: 2, y: 2, z: 4, core: 2. Of those that a mesh axis runs over, the one named last changes fastest.
Arguments:
- activations: bfloat16 [2, 8, 512, 4096], P(None, ('groups', 'rows'), 'seq'), parts along dimension 1, may hold values from -6 to 6
- out_grads: bfloat16 [2, 8, 512, 4096], P(None, ('groups', 'rows'), 'seq'), parts along dimension 1, may hold values from -6 to 6
- lengths: int32 [8], P(('groups', 'rows')), parts along dimension 0, may hold values from 64 to 512
- proj_in: bfloat16 [2, 4096, 64], replicated, may hold values from -0.09375 to 0.09375
- proj_out: bfloat16 [2, 4096, 64], replicated, may hold values from -0.09375 to 0.09375
- basis_in: float32 [2, 64, 64], replicated, may hold values from -0.75 to 0.75
- basis_out: float32 [2, 64, 64], replicated, may hold values from -0.75 to 0.75
- eigen: float32 [2, 64, 64], replicated, may hold values from 10 to 1000
- store: bfloat16 [1024, 8192], P(('groups', 'rows', 'seq')), parts along dimension 0, may hold values from -0.0625 to 0.0625
- candidates: int32 [8, 64], P('groups'), parts along dimension 0, may hold values from 0 to 511
Outputs:
- scores: float32 [1024, 4], P(('groups', 'rows', 'seq')), parts along dimension 0
- picked: float32 [8, 64], P('groups'), parts along dimension 0
The draws below stay inside these ranges and needn't reach their ends.
There are 2 independent parts, one for each index of `groups`. The reference program is written for one: setup_inputs(seed, part) draws one part's arguments, and reference() takes and returns one part's arrays. A program takes and returns all parts, laid end to end along the dimension named above; an argument that names none is the same for every part. Nothing has to cross between parts.
All inputs are finite; a program needn't handle non-finite values.
Results may differ from the reference program's by a relative error of at most 0.005.
Values may be sent and summed in bfloat16 or wider, within the bound.
A program may use at most 64 MiB of HBM per device.

```python
import math
import jax
import jax.numpy as jnp
from jax import lax

D = 4096
RANK = 64
NL = 2
TOPK = 64
BATCH = 4
LENGTH = 512
ROWS_TOTAL = 512
FLAT = 8192


def draw_lengths(key, part):
    first, second = jax.random.split(jax.random.fold_in(key, 7))
    base = jax.random.randint(first, (BATCH,), LENGTH // 8, LENGTH + 1)
    chosen = jax.random.randint(second, (), 0, BATCH)
    return jnp.where(jnp.arange(BATCH) == chosen, LENGTH, base).astype(jnp.int32)


def place_ends(entries, stream_key, least, largest):
    index_at = [jax.random.randint(jax.random.fold_in(stream_key, axis), (), 0, length) for axis, length in enumerate(entries.shape)]
    longest = entries.shape.index(max(entries.shape))
    next_to = index_at[:longest] + [(index_at[longest] + 1) % entries.shape[longest]] + index_at[longest + 1:]
    return entries.at[tuple(index_at)].set(least).at[tuple(next_to)].set(largest)


def block_levels(rng, extent, cuts, least, top_value):
    loudness = 1.0
    for position, parts in cuts:
        heights = jax.random.uniform(jax.random.fold_in(jax.random.fold_in(rng, 6), position), (parts,), jnp.float32, least / len(cuts), top_value / len(cuts))
        loudness = loudness * jnp.repeat(jnp.exp(heights), extent[position] // parts).reshape((-1,) + (1,) * (len(extent) - 1 - position))
    return loudness


def gaussian(stream_key, shape, deviation, bound, shards=(), kind=jnp.bfloat16):
    array = jax.random.normal(stream_key, shape, jnp.float32) * deviation
    if len(shards) > 0:
        array = block_levels(stream_key, shape, shards, -0.22, 0.18) * array
    return jnp.clip(array, min=-bound, max=bound).astype(kind)


def setup_inputs(seed: int = 0, part: int = 0) -> dict:
    keys = jax.random.split(jax.random.key(seed), 11)
    own_keys = jax.random.split(jax.random.fold_in(keys[10], part), 11)
    activations = gaussian(own_keys[0], (NL, BATCH, LENGTH, D), 1.0, 6.0, ((1, 4), (2, 4)))
    out_grads = gaussian(own_keys[1], (NL, BATCH, LENGTH, D), 1.0, 6.0, ((1, 4), (2, 4)))
    lengths = draw_lengths(jax.random.fold_in(jax.random.fold_in(keys[10], part), 71), part)
    proj_in = gaussian(keys[3], (NL, D, RANK), D ** -0.5, 0.09375)
    proj_out = gaussian(keys[4], (NL, D, RANK), D ** -0.5, 0.09375)
    basis_in = gaussian(keys[5], (NL, RANK, RANK), RANK ** -0.5, 0.75, (), jnp.float32)
    basis_out = gaussian(keys[6], (NL, RANK, RANK), RANK ** -0.5, 0.75, (), jnp.float32)
    eigen = jnp.clip(jnp.exp(jax.random.uniform(keys[7], (NL, RANK, RANK), jnp.float32, math.log(10.0), math.log(1000.0))), 10.0, 1000.0)
    store = gaussian(own_keys[8], (ROWS_TOTAL, FLAT), FLAT ** -0.5, 0.0625, ((0, 16),))
    candidates = place_ends(jax.random.randint(own_keys[9], (BATCH, TOPK), 0, ROWS_TOTAL), jax.random.fold_in(own_keys[9], 1), 0, ROWS_TOTAL - 1).astype(jnp.int32)
    return {"activations": activations, "out_grads": out_grads, "lengths": lengths, "proj_in": proj_in, "proj_out": proj_out, "basis_in": basis_in, "basis_out": basis_out, "eigen": eigen, "store": store, "candidates": candidates}


damping = 1.0


def reference(activations, out_grads, lengths, proj_in, proj_out, basis_in, basis_out, eigen, store, candidates):
    nl, batch, length, width = activations.shape
    positions = jnp.arange(length, dtype=jnp.int32)
    mask = (positions[None, :] < lengths[:, None]).astype(jnp.bfloat16)

    def layer(items):
        acts, grads, p_in, p_out = items
        pa = jnp.dot(acts.reshape(batch * length, width), p_in, preferred_element_type=jnp.float32)
        pg = jnp.dot(grads.reshape(batch * length, width), p_out, preferred_element_type=jnp.float32)
        pa = pa.astype(jnp.bfloat16).reshape(batch, length, -1) * mask[:, :, None]
        pg = pg.astype(jnp.bfloat16).reshape(batch, length, -1) * mask[:, :, None]
        return jnp.einsum('bto,bti->boi', pg.astype(jnp.float32), pa.astype(jnp.float32), precision=lax.Precision.HIGHEST)

    grad = lax.map(layer, (activations, out_grads, proj_in, proj_out))
    high = lax.Precision.HIGHEST
    rot = jnp.einsum('loj,lboi,lik->lbjk', basis_out, grad, basis_in, precision=high)
    pre = rot / (eigen[:, None] + damping)
    back = jnp.einsum('loj,lbjk,lik->lboi', basis_out, pre, basis_in, precision=high)
    test = jnp.transpose(back, (1, 0, 2, 3)).reshape(batch, -1).astype(jnp.bfloat16)
    scores = jnp.dot(store, test.T, preferred_element_type=jnp.float32)
    picked = scores[candidates, jnp.arange(batch, dtype=jnp.int32)[:, None]]
    return scores, picked
```

```python
import functools

import jax
import jax.numpy as jnp
from jax import lax
from jax.experimental import pallas as pl
from jax.experimental.pallas import tpu as pltpu
from jax.sharding import PartitionSpec as P

damping = 1.0
MESH = pl.DeviceIdType.MESH
F32 = jnp.float32
BF16 = jnp.bfloat16
NN = (((1,), (0,)), ((), ()))
NT = (((1,), (1,)), ((), ()))


def mm(a, b, dims=NN):
    return lax.dot_general(a, b, dims, preferred_element_type=F32)


def split(x):
    hi = x.astype(BF16)
    return hi, (x - hi.astype(F32)).astype(BF16)


def mm3(a, b, dims=NN):
    return mm(a[0], b[0], dims) + (mm(a[0], b[1], dims) + mm(a[1], b[0], dims))


def each(count, step):
    if count <= 16:
        for i in range(count):
            step(i)
    else:
        lax.fori_loop(0, count, lambda i, c: (step(i), c)[1], 0)


def kernel(
    nr, ns, lengths,
    acts_hbm, grads_hbm, pin_hbm, pout_hbm, bin_hbm, bout_hbm, eig_hbm, store_hbm, cand_hbm,
    scores_ref, picked_ref,
    acts, grads, pin, pout, bin_, bout, eig, store, cand,
    gsend, grecv, tsend, trecv, psend, precv,
    load_sem, small_sem, gs_sem, gr_sem, ts_sem, tr_sem, ps_sem, pr_sem,
):
    nl, tok, width = acts.shape
    rank = pin.shape[1]
    rdev = store.shape[0]
    half = rank // 2
    n = nr * ns
    row, seq = lax.axis_index("rows"), lax.axis_index("seq")
    me = row * ns + seq

    loads = []
    for l in range(nl):
        loads.append([
            pltpu.make_async_copy(src, dst, load_sem.at[l, i])
            for i, (src, dst) in enumerate((
                (pin_hbm.at[l], pin.at[l]),
                (acts_hbm.at[l, 0], acts.at[l]),
                (pout_hbm.at[l], pout.at[l]),
                (grads_hbm.at[l, 0], grads.at[l]),
            ))
        ])
    small = [
        pltpu.make_async_copy(src, dst, small_sem.at[i])
        for i, (src, dst) in enumerate((
            (bin_hbm, bin_), (bout_hbm, bout), (eig_hbm, eig), (cand_hbm, cand), (store_hbm, store),
        ))
    ]
    for c in small[:4]:
        c.start()
    for group in loads:
        for c in group:
            c.start()
    small[4].start()

    barrier = pltpu.get_barrier_semaphore()

    def peer(e):
        to = lax.rem(me + e + 1, n)
        return {"rows": to // ns, "seq": lax.rem(to, ns)}

    each(n - 1, lambda e: pl.semaphore_signal(
        barrier, inc=1, device_id=peer(e), device_id_type=MESH))

    for c in small[:3]:
        c.wait()
    i0 = lax.broadcasted_iota(jnp.int32, (rank, rank), 0)
    i1 = lax.broadcasted_iota(jnp.int32, (rank, rank), 1)
    order = (i1 == jnp.where(i0 < half, 2 * i0, 2 * (i0 - half) + 1)).astype(BF16)
    bi, bi2, bot, beo = [], [], [], []
    for l in range(nl):
        b = split(bin_[l])
        bi.append(b)
        bi2.append(tuple(jnp.concatenate([x, x], axis=0) for x in b))
        bot.append(split(jnp.transpose(bout[l])))
        beo.append(tuple(mm(order, x).astype(BF16) for x in split(bout[l])))

    pos = seq * tok + lax.broadcasted_iota(jnp.int32, (tok, rank), 0)
    keep = pos < lengths[0]

    def gcopy(l, d):
        return pltpu.make_async_remote_copy(
            src_ref=gsend.at[l], dst_ref=grecv.at[l, d],
            send_sem=gs_sem.at[l, d], recv_sem=gr_sem.at[l, d],
            device_id={"seq": lax.rem(seq + d + 1, ns)}, device_id_type=MESH)

    own = []
    for l in range(nl):
        loads[l][0].wait()
        loads[l][1].wait()
        pa = mm(acts[l], pin[l], NT).astype(BF16)
        pa = jnp.where(keep, pa.astype(F32), 0.0).astype(BF16)
        loads[l][2].wait()
        loads[l][3].wait()
        pgt = mm(pout[l], grads[l], NT).astype(BF16)
        g = mm(pgt, pa)
        own.append(g)
        gsend[l] = g.astype(BF16)
        if l == 0:
            pl.semaphore_wait(barrier, n - 1)
        each(ns - 1, lambda d: gcopy(l, d).start())

    tests = []
    for l in range(nl):
        total = own[l]
        for d in range(ns - 1):
            gcopy(l, d).wait_recv()
            total = total + grecv[l, d].astype(F32)
        y = mm3(split(total), bi[l])
        rot = mm3(bot[l], split(y))
        pre = rot / (eig[l] + damping)
        x2 = mm3(split(pre), bi2[l], NT)
        z = mm3(beo[l], split(x2))
        lane = lax.broadcasted_iota(jnp.int32, (half, 2 * rank), 1)
        t = jnp.where(lane < rank, z[:half], z[half:]).astype(BF16)
        tsend[pl.ds(l * half, half), :] = t
        tests.append(t)

    def tcopy(d):
        return pltpu.make_async_remote_copy(
            src_ref=tsend, dst_ref=trecv.at[d],
            send_sem=ts_sem.at[d], recv_sem=tr_sem.at[d],
            device_id={"rows": lax.rem(row + d + 1, nr)}, device_id_type=MESH)

    each(nr - 1, lambda d: tcopy(d).start())

    for c in small[3:]:
        c.wait()
    lanes = 2 * rank
    chunks = nl * half
    eye = lax.broadcasted_iota(jnp.int32, (rdev, rdev), 0) == lax.broadcasted_iota(
        jnp.int32, (rdev, rdev), 1)
    rows_k = me * rdev + lax.broadcasted_iota(jnp.int32, (rdev, cand.shape[1]), 0)

    def score(t, b):
        acc = [jnp.zeros((rdev, lanes), F32) for _ in range(2)]
        for c in range(chunks):
            s = store[:, c * lanes:(c + 1) * lanes].astype(F32)
            acc[c % 2] = acc[c % 2] + s * t[c:c + 1, :]
        col = jnp.sum(acc[0] + acc[1], axis=1, keepdims=True)
        scores_ref[pl.ds(b, 1), :] = jnp.sum(jnp.where(eye, col, 0.0), axis=0, keepdims=True)
        hit = cand[pl.ds(b, 1), :] == rows_k
        psend[pl.ds(b, 1), :] = jnp.sum(jnp.where(hit, col, 0.0), axis=0, keepdims=True)

    score(tsend[...].astype(F32), row)

    def other(d):
        tcopy(d).wait_recv()
        score(trecv[d].astype(F32), lax.rem(row + nr - d - 1, nr))

    each(nr - 1, other)

    def pcopy(e):
        return pltpu.make_async_remote_copy(
            src_ref=psend, dst_ref=precv.at[e],
            send_sem=ps_sem.at[e], recv_sem=pr_sem.at[e],
            device_id=peer(e), device_id_type=MESH)

    each(n - 1, lambda e: pcopy(e).start())
    picked_ref[...] = psend[...]

    for l in range(nl):
        each(ns - 1, lambda d: gcopy(l, d).wait_send())
    each(nr - 1, lambda d: tcopy(d).wait_send())

    def add(e):
        pcopy(e).wait_recv()
        picked_ref[...] += precv[e]

    each(n - 1, add)
    each(n - 1, lambda e: pcopy(e).wait_send())


def body(nr, ns, activations, out_grads, lengths, proj_in, proj_out,
         basis_in, basis_out, eigen, store, candidates):
    nl, _, tok, width = activations.shape
    rank = proj_in.shape[2]
    rdev, flat = store.shape
    batch, topk = candidates.shape
    n = nr * ns
    dma = pltpu.SemaphoreType.DMA
    vm = pltpu.VMEM
    hbm = pl.BlockSpec(memory_space=pl.ANY)
    scores, picked = pl.pallas_call(
        functools.partial(kernel, nr, ns),
        out_shape=(
            jax.ShapeDtypeStruct((batch, rdev), F32),
            jax.ShapeDtypeStruct((batch, topk), F32),
        ),
        in_specs=[pl.BlockSpec(memory_space=pltpu.SMEM)] + [hbm] * 9,
        out_specs=(pl.BlockSpec(memory_space=pltpu.VMEM),) * 2,
        scratch_shapes=[
            vm((nl, tok, width), BF16), vm((nl, tok, width), BF16),
            vm((nl, rank, width), BF16), vm((nl, rank, width), BF16),
            vm((nl, rank, rank), F32), vm((nl, rank, rank), F32), vm((nl, rank, rank), F32),
            vm((rdev, flat), BF16), vm((batch, topk), jnp.int32),
            vm((nl, rank, rank), BF16), vm((nl, ns - 1, rank, rank), BF16),
            vm((nl * rank // 2, 2 * rank), BF16), vm((nr - 1, nl * rank // 2, 2 * rank), BF16),
            vm((batch, topk), F32), vm((n - 1, batch, topk), F32),
            dma((nl, 4)), dma((5,)),
            dma((nl, ns - 1)), dma((nl, ns - 1)),
            dma((nr - 1,)), dma((nr - 1,)),
            dma((n - 1,)), dma((n - 1,)),
        ],
        compiler_params=pltpu.CompilerParams(
            collective_id=0, has_side_effects=True, vmem_limit_bytes=32 * 2**20),
    )(
        lengths, activations, out_grads,
        jnp.swapaxes(proj_in, 1, 2), jnp.swapaxes(proj_out, 1, 2),
        basis_in, basis_out, eigen, store, candidates,
    )
    return scores.T, picked


def solution(mesh):
    placed = (
        P(None, ("groups", "rows"), "seq", None),
        P(None, ("groups", "rows"), "seq", None),
        P(("groups", "rows")),
        P(),
        P(),
        P(),
        P(),
        P(),
        P(("groups", "rows", "seq"), None),
        P("groups", None),
    )
    return jax.shard_map(
        functools.partial(body, mesh.shape["rows"], mesh.shape["seq"]),
        mesh=mesh,
        in_specs=placed,
        out_specs=(P(("groups", "rows", "seq"), None), P("groups", None)),
        check_vma=False,
    )
```

```python
import functools

import jax
import jax.numpy as jnp
from jax import lax
from jax.experimental import pallas as pl
from jax.experimental.pallas import tpu as pltpu
from jax.sharding import PartitionSpec as P

damping = 1.0
MESH = pl.DeviceIdType.MESH
F32 = jnp.float32
BF16 = jnp.bfloat16
NN = (((1,), (0,)), ((), ()))
NT = (((1,), (1,)), ((), ()))


def mm(a, b, dims=NN):
    return lax.dot_general(a, b, dims, preferred_element_type=F32)


def split(x):
    hi = x.astype(BF16)
    return hi, (x - hi.astype(F32)).astype(BF16)


def mm3(a, b, dims=NN):
    return mm(a[0], b[0], dims) + (mm(a[0], b[1], dims) + mm(a[1], b[0], dims))


def each(count, step):
    if count <= 16:
        for i in range(count):
            step(i)
    else:
        lax.fori_loop(0, count, lambda i, c: (step(i), c)[1], 0)


def kernel(
    nr, ns, lengths,
    acts_hbm, grads_hbm, pin_hbm, pout_hbm, bin_hbm, bout_hbm, eig_hbm, store_hbm, cand_hbm,
    scores_ref, picked_ref,
    acts, grads, pin, pout, bin_, bout, eig, store, cand,
    gsend, grecv, tsend, trecv, psend, precv,
    load_sem, small_sem, gs_sem, gr_sem, ts_sem, tr_sem, ps_sem, pr_sem,
):
    nl, tok, width = acts.shape
    rank = pin.shape[1]
    rdev = store.shape[0]
    half = rank // 2
    n = nr * ns
    row, seq = lax.axis_index("rows"), lax.axis_index("seq")
    me = row * ns + seq

    loads = []
    for l in range(nl):
        loads.append([
            pltpu.make_async_copy(src, dst, load_sem.at[l, i])
            for i, (src, dst) in enumerate((
                (pin_hbm.at[l], pin.at[l]),
                (acts_hbm.at[l, 0], acts.at[l]),
                (pout_hbm.at[l], pout.at[l]),
                (grads_hbm.at[l, 0], grads.at[l]),
            ))
        ])
    small = [
        pltpu.make_async_copy(src, dst, small_sem.at[i])
        for i, (src, dst) in enumerate((
            (bin_hbm, bin_), (bout_hbm, bout), (eig_hbm, eig), (cand_hbm, cand), (store_hbm, store),
        ))
    ]
    for c in small[:4]:
        c.start()
    for group in loads:
        for c in group:
            c.start()
    small[4].start()

    barrier = pltpu.get_barrier_semaphore()

    def peer(e):
        to = lax.rem(me + e + 1, n)
        return {"rows": to // ns, "seq": lax.rem(to, ns)}

    each(n - 1, lambda e: pl.semaphore_signal(
        barrier, inc=1, device_id=peer(e), device_id_type=MESH))

    for c in small[:3]:
        c.wait()
    i0 = lax.broadcasted_iota(jnp.int32, (rank, rank), 0)
    i1 = lax.broadcasted_iota(jnp.int32, (rank, rank), 1)
    order = (i1 == jnp.where(i0 < half, 2 * i0, 2 * (i0 - half) + 1)).astype(BF16)
    bi, bi2, bot, beo = [], [], [], []
    for l in range(nl):
        b = split(bin_[l])
        bi.append(b)
        bi2.append(tuple(jnp.concatenate([x, x], axis=0) for x in b))
        bot.append(split(jnp.transpose(bout[l])))
        beo.append(tuple(mm(order, x).astype(BF16) for x in split(bout[l])))

    pos = seq * tok + lax.broadcasted_iota(jnp.int32, (tok, rank), 0)
    keep = pos < lengths[0]

    def gcopy(l, d):
        return pltpu.make_async_remote_copy(
            src_ref=gsend.at[l], dst_ref=grecv.at[l, d],
            send_sem=gs_sem.at[l, d], recv_sem=gr_sem.at[l, d],
            device_id={"seq": lax.rem(seq + d + 1, ns)}, device_id_type=MESH)

    own = []
    for l in range(nl):
        loads[l][0].wait()
        loads[l][1].wait()
        pa = mm(acts[l], pin[l], NT).astype(BF16)
        pa = jnp.where(keep, pa.astype(F32), 0.0).astype(BF16)
        loads[l][2].wait()
        loads[l][3].wait()
        pgt = mm(pout[l], grads[l], NT).astype(BF16)
        g = mm(pgt, pa)
        own.append(g)
        gsend[l] = g.astype(BF16)
        if l == 0:
            pl.semaphore_wait(barrier, n - 1)
        each(ns - 1, lambda d: gcopy(l, d).start())

    tests = []
    for l in range(nl):
        total = own[l]
        for d in range(ns - 1):
            gcopy(l, d).wait_recv()
            total = total + grecv[l, d].astype(F32)
        y = mm3(split(total), bi[l])
        rot = mm3(bot[l], split(y))
        pre = rot / (eig[l] + damping)
        x2 = mm3(split(pre), bi2[l], NT)
        z = mm3(beo[l], split(x2))
        lane = lax.broadcasted_iota(jnp.int32, (half, 2 * rank), 1)
        t = jnp.where(lane < rank, z[:half], z[half:]).astype(BF16)
        tsend[pl.ds(l * half, half), :] = t
        tests.append(t)

    def tcopy(d):
        return pltpu.make_async_remote_copy(
            src_ref=tsend, dst_ref=trecv.at[d],
            send_sem=ts_sem.at[d], recv_sem=tr_sem.at[d],
            device_id={"rows": lax.rem(row + d + 1, nr)}, device_id_type=MESH)

    each(nr - 1, lambda d: tcopy(d).start())

    for c in small[3:]:
        c.wait()
    lanes = 2 * rank
    chunks = nl * half
    eye = lax.broadcasted_iota(jnp.int32, (rdev, rdev), 0) == lax.broadcasted_iota(
        jnp.int32, (rdev, rdev), 1)
    rows_k = me * rdev + lax.broadcasted_iota(jnp.int32, (rdev, cand.shape[1]), 0)

    def score(t, b):
        acc = [jnp.zeros((rdev, lanes), F32) for _ in range(2)]
        for c in range(chunks):
            s = store[:, c * lanes:(c + 1) * lanes].astype(F32)
            acc[c % 2] = acc[c % 2] + s * t[c:c + 1, :]
        col = jnp.sum(acc[0] + acc[1], axis=1, keepdims=True)
        scores_ref[pl.ds(b, 1), :] = jnp.sum(jnp.where(eye, col, 0.0), axis=0, keepdims=True)
        hit = cand[pl.ds(b, 1), :] == rows_k
        psend[pl.ds(b, 1), :] = jnp.sum(jnp.where(hit, col, 0.0), axis=0, keepdims=True)

    score(tsend[...].astype(F32), row)

    def other(d):
        tcopy(d).wait_recv()
        score(trecv[d].astype(F32), lax.rem(row + nr - d - 1, nr))

    each(nr - 1, other)

    def pcopy(e):
        return pltpu.make_async_remote_copy(
            src_ref=psend, dst_ref=precv.at[e],
            send_sem=ps_sem.at[e], recv_sem=pr_sem.at[e],
            device_id=peer(e), device_id_type=MESH)

    each(n - 1, lambda e: pcopy(e).start())
    picked_ref[...] = psend[...]

    for l in range(nl):
        each(ns - 1, lambda d: gcopy(l, d).wait_send())
    each(nr - 1, lambda d: tcopy(d).wait_send())

    def add(e):
        pcopy(e).wait_recv()
        picked_ref[...] += precv[e]

    each(n - 1, add)
    each(n - 1, lambda e: pcopy(e).wait_send())


def body(nr, ns, activations, out_grads, lengths, proj_in, proj_out,
         basis_in, basis_out, eigen, store, candidates):
    nl, _, tok, width = activations.shape
    rank = proj_in.shape[2]
    rdev, flat = store.shape
    batch, topk = candidates.shape
    n = nr * ns
    dma = pltpu.SemaphoreType.DMA
    vm = pltpu.VMEM
    hbm = pl.BlockSpec(memory_space=pltpu.HBM)
    scores, picked = pl.pallas_call(
        functools.partial(kernel, nr, ns),
        out_shape=(
            jax.ShapeDtypeStruct((batch, rdev), F32),
            jax.ShapeDtypeStruct((batch, topk), F32),
        ),
        in_specs=[pl.BlockSpec(memory_space=pltpu.SMEM)] + [hbm] * 9,
        out_specs=(pl.BlockSpec(memory_space=pltpu.VMEM),) * 2,
        scratch_shapes=[
            vm((nl, tok, width), BF16), vm((nl, tok, width), BF16),
            vm((nl, rank, width), BF16), vm((nl, rank, width), BF16),
            vm((nl, rank, rank), F32), vm((nl, rank, rank), F32), vm((nl, rank, rank), F32),
            vm((rdev, flat), BF16), vm((batch, topk), jnp.int32),
            vm((nl, rank, rank), BF16), vm((nl, ns - 1, rank, rank), BF16),
            vm((nl * rank // 2, 2 * rank), BF16), vm((nr - 1, nl * rank // 2, 2 * rank), BF16),
            vm((batch, topk), F32), vm((n - 1, batch, topk), F32),
            dma((nl, 4)), dma((5,)),
            dma((nl, ns - 1)), dma((nl, ns - 1)),
            dma((nr - 1,)), dma((nr - 1,)),
            dma((n - 1,)), dma((n - 1,)),
        ],
        compiler_params=pltpu.CompilerParams(
            collective_id=0, has_side_effects=True, vmem_limit_bytes=60 * 2**20),
    )(
        lengths, activations, out_grads,
        jnp.swapaxes(proj_in, 1, 2), jnp.swapaxes(proj_out, 1, 2),
        basis_in, basis_out, eigen, store, candidates,
    )
    return scores.T, picked


def solution(mesh):
    placed = (
        P(None, ("groups", "rows"), "seq", None),
        P(None, ("groups", "rows"), "seq", None),
        P(("groups", "rows")),
        P(),
        P(),
        P(),
        P(),
        P(),
        P(("groups", "rows", "seq"), None),
        P("groups", None),
    )
    return jax.shard_map(
        functools.partial(body, mesh.shape["rows"], mesh.shape["seq"]),
        mesh=mesh,
        in_specs=placed,
        out_specs=(P(("groups", "rows", "seq"), None), P("groups", None)),
        check_vma=False,
    )
```

```python
import functools

import jax
import jax.numpy as jnp
from jax import lax
from jax.experimental import pallas as pl
from jax.experimental.pallas import tpu as pltpu
from jax.sharding import PartitionSpec as P

damping = 1.0
MESH = pl.DeviceIdType.MESH
F32 = jnp.float32
BF16 = jnp.bfloat16
NN = (((1,), (0,)), ((), ()))
NT = (((1,), (1,)), ((), ()))


def mm(a, b, dims=NN):
    return lax.dot_general(a, b, dims, preferred_element_type=F32)


def split(x):
    hi = x.astype(BF16)
    return hi, (x - hi.astype(F32)).astype(BF16)


def mm3(a, b, dims=NN):
    return mm(a[0], b[0], dims) + (mm(a[0], b[1], dims) + mm(a[1], b[0], dims))


def each(count, step):
    if count <= 16:
        for i in range(count):
            step(i)
    else:
        lax.fori_loop(0, count, lambda i, c: (step(i), c)[1], 0)


def kernel(
    nr, ns, lengths,
    acts_hbm, grads_hbm, pin_hbm, pout_hbm, bin_hbm, bout_hbm, eig_hbm, store_hbm, cand_hbm,
    scores_ref, picked_ref,
    acts, grads, pin, pout, bin_, bout, eig, store, cand,
    gsend, grecv, tsend, trecv, psend, precv,
    load_sem, small_sem, gs_sem, gr_sem, ts_sem, tr_sem, ps_sem, pr_sem,
):
    nl, tok, width = acts.shape
    rank = pin.shape[1]
    rdev = store.shape[0]
    half = rank // 2
    n = nr * ns
    row, seq = lax.axis_index("rows"), lax.axis_index("seq")
    me = row * ns + seq

    loads = []
    for l in range(nl):
        loads.append([
            pltpu.make_async_copy(src, dst, load_sem.at[l, i])
            for i, (src, dst) in enumerate((
                (pin_hbm.at[l], pin.at[l]),
                (acts_hbm.at[l, 0], acts.at[l]),
                (pout_hbm.at[l], pout.at[l]),
                (grads_hbm.at[l, 0], grads.at[l]),
            ))
        ])
    small = [
        pltpu.make_async_copy(src, dst, small_sem.at[i])
        for i, (src, dst) in enumerate((
            (bin_hbm, bin_), (bout_hbm, bout), (eig_hbm, eig), (cand_hbm, cand), (store_hbm, store),
        ))
    ]
    for c in small[:4]:
        c.start()
    for group in loads:
        for c in group:
            c.start()
    small[4].start()

    barrier = pltpu.get_barrier_semaphore()

    def peer(e):
        to = lax.rem(me + e + 1, n)
        return {"rows": to // ns, "seq": lax.rem(to, ns)}

    each(ns - 1, lambda d: pl.semaphore_signal(
        barrier, inc=1, device_id={"seq": lax.rem(seq + d + 1, ns)}, device_id_type=MESH))
    each(nr - 1, lambda d: pl.semaphore_signal(
        barrier, inc=1, device_id={"rows": lax.rem(row + d + 1, nr)}, device_id_type=MESH))

    for c in small[:3]:
        c.wait()
    i0 = lax.broadcasted_iota(jnp.int32, (rank, rank), 0)
    i1 = lax.broadcasted_iota(jnp.int32, (rank, rank), 1)
    order = (i1 == jnp.where(i0 < half, 2 * i0, 2 * (i0 - half) + 1)).astype(BF16)
    bi, bi2, bot, beo = [], [], [], []
    for l in range(nl):
        b = split(bin_[l])
        bi.append(b)
        bi2.append(tuple(jnp.concatenate([x, x], axis=0) for x in b))
        bot.append(split(jnp.transpose(bout[l])))
        beo.append(tuple(mm(order, x).astype(BF16) for x in split(bout[l])))

    pos = seq * tok + lax.broadcasted_iota(jnp.int32, (tok, rank), 0)
    keep = pos < lengths[0]

    def gcopy(l, d):
        return pltpu.make_async_remote_copy(
            src_ref=gsend.at[l], dst_ref=grecv.at[l, d],
            send_sem=gs_sem.at[l, d], recv_sem=gr_sem.at[l, d],
            device_id={"seq": lax.rem(seq + d + 1, ns)}, device_id_type=MESH)

    low = lax.broadcasted_iota(jnp.int32, (half, 2 * rank), 1) < rank
    own = []
    for l in range(nl):
        loads[l][0].wait()
        loads[l][1].wait()
        pa = mm(acts[l], pin[l], NT).astype(BF16)
        pa = jnp.where(keep, pa.astype(F32), 0.0).astype(BF16)
        loads[l][2].wait()
        loads[l][3].wait()
        pgt = mm(pout[l], grads[l], NT).astype(BF16)
        g = mm(pgt, jnp.concatenate([pa, pa], axis=1))
        g = jnp.where(low, g[:half], g[half:])
        own.append(g)
        gsend[l] = g.astype(BF16)
        if l == 0:
            pl.semaphore_wait(barrier, ns + nr - 2)
        each(ns - 1, lambda d: gcopy(l, d).start())

    tests = []
    for l in range(nl):
        total = own[l]
        for d in range(ns - 1):
            gcopy(l, d).wait_recv()
            total = total + grecv[l, d].astype(F32)
        total = jnp.concatenate([total[:, :rank], total[:, rank:]], axis=0)
        y = mm3(split(total), bi[l])
        rot = mm3(bot[l], split(y))
        pre = rot / (eig[l] + damping)
        x2 = mm3(split(pre), bi2[l], NT)
        z = mm3(beo[l], split(x2))
        t = jnp.where(low, z[:half], z[half:]).astype(BF16)
        tsend[pl.ds(l * half, half), :] = t
        tests.append(t)

    def tcopy(d):
        return pltpu.make_async_remote_copy(
            src_ref=tsend, dst_ref=trecv.at[d],
            send_sem=ts_sem.at[d], recv_sem=tr_sem.at[d],
            device_id={"rows": lax.rem(row + d + 1, nr)}, device_id_type=MESH)

    each(nr - 1, lambda d: tcopy(d).start())

    for c in small[3:]:
        c.wait()
    lanes = 2 * rank
    chunks = nl * half
    eye = lax.broadcasted_iota(jnp.int32, (rdev, rdev), 0) == lax.broadcasted_iota(
        jnp.int32, (rdev, rdev), 1)
    rows_k = me * rdev + lax.broadcasted_iota(jnp.int32, (rdev, cand.shape[1]), 0)

    def score(t, b):
        acc = [jnp.zeros((rdev, lanes), F32) for _ in range(2)]
        for c in range(chunks):
            s = store[:, c * lanes:(c + 1) * lanes].astype(F32)
            acc[c % 2] = acc[c % 2] + s * t[c:c + 1, :]
        col = jnp.sum(acc[0] + acc[1], axis=1, keepdims=True)
        scores_ref[pl.ds(b, 1), :] = jnp.sum(jnp.where(eye, col, 0.0), axis=0, keepdims=True)
        hit = cand[pl.ds(b, 1), :] == rows_k
        psend[pl.ds(b, 1), :] = jnp.sum(jnp.where(hit, col, 0.0), axis=0, keepdims=True)

    score(tsend[...].astype(F32), row)

    def other(d):
        tcopy(d).wait_recv()
        score(trecv[d].astype(F32), lax.rem(row + nr - d - 1, nr))

    each(nr - 1, other)

    def pcopy(e):
        return pltpu.make_async_remote_copy(
            src_ref=psend, dst_ref=precv.at[e],
            send_sem=ps_sem.at[0], recv_sem=pr_sem.at[0],
            device_id=peer(e), device_id_type=MESH)

    each(n - 1, lambda e: pcopy(e).start())
    for l in range(nl):
        each(ns - 1, lambda d: gcopy(l, d).wait_send())
    each(nr - 1, lambda d: tcopy(d).wait_send())

    pltpu.make_async_copy(precv, precv, pr_sem.at[0]).wait()
    picked_ref[...] = psend[...] + jnp.sum(precv[...], axis=0)
    pltpu.make_async_copy(precv, precv, ps_sem.at[0]).wait()


def body(nr, ns, activations, out_grads, lengths, proj_in, proj_out,
         basis_in, basis_out, eigen, store, candidates):
    nl, _, tok, width = activations.shape
    rank = proj_in.shape[2]
    rdev, flat = store.shape
    batch, topk = candidates.shape
    n = nr * ns
    dma = pltpu.SemaphoreType.DMA
    vm = pltpu.VMEM
    hbm = pl.BlockSpec(memory_space=pltpu.HBM)
    scores, picked = pl.pallas_call(
        functools.partial(kernel, nr, ns),
        out_shape=(pltpu.VMEM((batch, rdev), F32), pltpu.VMEM((batch, topk), F32)),
        in_specs=[pl.BlockSpec(memory_space=pltpu.SMEM)] + [hbm] * 9,
        out_specs=(pl.BlockSpec(memory_space=pltpu.VMEM),) * 2,
        scratch_shapes=[
            vm((nl, tok, width), BF16), vm((nl, tok, width), BF16),
            vm((nl, rank, width), BF16), vm((nl, rank, width), BF16),
            vm((nl, rank, rank), F32), vm((nl, rank, rank), F32), vm((nl, rank, rank), F32),
            vm((rdev, flat), BF16), vm((batch, topk), jnp.int32),
            vm((nl, rank // 2, 2 * rank), BF16), vm((nl, ns - 1, rank // 2, 2 * rank), BF16),
            vm((nl * rank // 2, 2 * rank), BF16), vm((nr - 1, nl * rank // 2, 2 * rank), BF16),
            vm((batch, topk), F32), vm((n - 1, batch, topk), F32),
            dma((nl, 4)), dma((5,)),
            dma((nl, ns - 1)), dma((nl, ns - 1)),
            dma((nr - 1,)), dma((nr - 1,)),
            dma((1,)), dma((1,)),
        ],
        compiler_params=pltpu.CompilerParams(
            collective_id=0, has_side_effects=True, vmem_limit_bytes=60 * 2**20),
    )(
        lengths, activations, out_grads,
        jnp.swapaxes(proj_in, 1, 2), jnp.swapaxes(proj_out, 1, 2),
        basis_in, basis_out, eigen, store, candidates,
    )
    return scores.T, picked


def solution(mesh):
    placed = (
        P(None, ("groups", "rows"), "seq", None),
        P(None, ("groups", "rows"), "seq", None),
        P(("groups", "rows")),
        P(),
        P(),
        P(),
        P(),
        P(),
        P(("groups", "rows", "seq"), None),
        P("groups", None),
    )
    return jax.shard_map(
        functools.partial(body, mesh.shape["rows"], mesh.shape["seq"]),
        mesh=mesh,
        in_specs=placed,
        out_specs=(P(("groups", "rows", "seq"), None), P("groups", None)),
        check_vma=False,
    )
```

```python
import functools

import jax
import jax.numpy as jnp
from jax import lax
from jax.experimental import pallas as pl
from jax.experimental.pallas import tpu as pltpu
from jax.sharding import PartitionSpec as P

damping = 1.0
MESH = pl.DeviceIdType.MESH
F32 = jnp.float32
BF16 = jnp.bfloat16
NN = (((1,), (0,)), ((), ()))
NT = (((1,), (1,)), ((), ()))


def mm(a, b, dims=NN):
    return lax.dot_general(a, b, dims, preferred_element_type=F32)


def split(x):
    hi = x.astype(BF16)
    return hi, (x - hi.astype(F32)).astype(BF16)


def mm3(a, b, dims=NN):
    return mm(a[0], b[0], dims) + (mm(a[0], b[1], dims) + mm(a[1], b[0], dims))


def each(count, step):
    if count <= 16:
        for i in range(count):
            step(i)
    else:
        lax.fori_loop(0, count, lambda i, c: (step(i), c)[1], 0)


def kernel(
    nr, ns, lengths,
    acts_hbm, grads_hbm, pin_hbm, pout_hbm, bin_hbm, bout_hbm, eig_hbm, store_hbm, cand_hbm,
    scores_ref, picked_ref,
    acts, grads, pin, pout, bin_, bout, eig, store, cand,
    gsend, grecv, tsend, trecv, psend, precv,
    load_sem, small_sem, gs_sem, gr_sem, ts_sem, tr_sem, ps_sem, pr_sem,
):
    nl, tok, width = acts.shape
    rank = pin.shape[1]
    rdev = store.shape[0]
    half = rank // 2
    n = nr * ns
    row, seq = lax.axis_index("rows"), lax.axis_index("seq")
    me = row * ns + seq

    loads = []
    for l in range(nl):
        loads.append([
            pltpu.make_async_copy(src, dst, load_sem.at[l, i])
            for i, (src, dst) in enumerate((
                (pin_hbm.at[l], pin.at[l]),
                (acts_hbm.at[l, 0], acts.at[l]),
                (pout_hbm.at[l], pout.at[l]),
                (grads_hbm.at[l, 0], grads.at[l]),
            ))
        ])
    small = [
        pltpu.make_async_copy(src, dst, small_sem.at[i])
        for i, (src, dst) in enumerate((
            (bin_hbm, bin_), (bout_hbm, bout), (eig_hbm, eig), (cand_hbm, cand), (store_hbm, store),
        ))
    ]
    for c in small[:4]:
        c.start()
    for group in loads:
        for c in group:
            c.start()
    small[4].start()

    barrier = pltpu.get_barrier_semaphore()

    def peer(e):
        to = lax.rem(me + e + 1, n)
        return {"rows": to // ns, "seq": lax.rem(to, ns)}

    each(ns - 1, lambda d: pl.semaphore_signal(
        barrier, inc=1, device_id={"seq": lax.rem(seq + d + 1, ns)}, device_id_type=MESH))
    each(nr - 1, lambda d: pl.semaphore_signal(
        barrier, inc=1, device_id={"rows": lax.rem(row + d + 1, nr)}, device_id_type=MESH))

    for c in small[:3]:
        c.wait()
    i0 = lax.broadcasted_iota(jnp.int32, (rank, rank), 0)
    i1 = lax.broadcasted_iota(jnp.int32, (rank, rank), 1)
    order = (i1 == jnp.where(i0 < half, 2 * i0, 2 * (i0 - half) + 1)).astype(BF16)
    bi, bi2, bot, beo = [], [], [], []
    for l in range(nl):
        b = split(bin_[l])
        bi.append(b)
        bi2.append(tuple(jnp.concatenate([x, x], axis=0) for x in b))
        bot.append(split(jnp.transpose(bout[l])))
        beo.append(tuple(mm(order, x).astype(BF16) for x in split(bout[l])))

    pos = seq * tok + lax.broadcasted_iota(jnp.int32, (tok, rank), 0)
    keep = pos < lengths[0]

    def gcopy(l, d):
        return pltpu.make_async_remote_copy(
            src_ref=gsend.at[l], dst_ref=grecv.at[l, d],
            send_sem=gs_sem.at[l, d], recv_sem=gr_sem.at[l, d],
            device_id={"seq": lax.rem(seq + d + 1, ns)}, device_id_type=MESH)

    low = lax.broadcasted_iota(jnp.int32, (half, 2 * rank), 1) < rank
    own = []
    for l in range(nl):
        loads[l][0].wait()
        loads[l][1].wait()
        pa = mm(acts[l], pin[l], NT).astype(BF16)
        pa = jnp.where(keep, pa.astype(F32), 0.0).astype(BF16)
        loads[l][2].wait()
        loads[l][3].wait()
        pgt = mm(pout[l], grads[l], NT).astype(BF16)
        g = mm(pgt, jnp.concatenate([pa, pa], axis=1))
        g = jnp.where(low, g[:half], g[half:])
        own.append(g)
        gsend[l] = g.astype(BF16)
        if l == 0:
            pl.semaphore_wait(barrier, ns + nr - 2)
        each(ns - 1, lambda d: gcopy(l, d).start())

    def tcopy(l, d):
        part = pl.ds(l * half, half)
        return pltpu.make_async_remote_copy(
            src_ref=tsend.at[part], dst_ref=trecv.at[d, part],
            send_sem=ts_sem.at[l, d], recv_sem=tr_sem.at[l, d],
            device_id={"rows": lax.rem(row + d + 1, nr)}, device_id_type=MESH)

    for l in range(nl):
        total = own[l]
        for d in range(ns - 1):
            gcopy(l, d).wait_recv()
            total = total + grecv[l, d].astype(F32)
        total = jnp.concatenate([total[:, :rank], total[:, rank:]], axis=0)
        y = mm3(split(total), bi[l])
        rot = mm3(bot[l], split(y))
        pre = rot / (eig[l] + damping)
        x2 = mm3(split(pre), bi2[l], NT)
        z = mm3(beo[l], split(x2))
        t = jnp.where(low, z[:half], z[half:]).astype(BF16)
        tsend[pl.ds(l * half, half), :] = t
        each(nr - 1, lambda d: tcopy(l, d).start())

    for c in small[3:]:
        c.wait()
    lanes = 2 * rank
    eye = lax.broadcasted_iota(jnp.int32, (rdev, rdev), 0) == lax.broadcasted_iota(
        jnp.int32, (rdev, rdev), 1)
    rows_k = me * rdev + lax.broadcasted_iota(jnp.int32, (rdev, cand.shape[1]), 0)

    def partial(t, l):
        t = t.astype(F32)
        acc = [jnp.zeros((rdev, lanes), F32) for _ in range(2)]
        for c in range(half):
            at = (l * half + c) * lanes
            s = store[:, at:at + lanes].astype(F32)
            acc[c % 2] = acc[c % 2] + s * t[c:c + 1, :]
        return acc[0] + acc[1]

    sums = [None] * nr
    for l in range(nl):
        part = pl.ds(l * half, half)
        for p in range(nr):
            if p > 0:
                tcopy(l, p - 1).wait_recv()
            a = partial(tsend[part, :] if p == 0 else trecv[p - 1, part, :], l)
            sums[p] = a if l == 0 else sums[p] + a
            if l == nl - 1:
                b = lax.rem(row + nr - p, nr)
                col = jnp.sum(sums[p], axis=1, keepdims=True)
                scores_ref[pl.ds(b, 1), :] = jnp.sum(
                    jnp.where(eye, col, 0.0), axis=0, keepdims=True)
                hit = cand[pl.ds(b, 1), :] == rows_k
                psend[pl.ds(b, 1), :] = jnp.sum(
                    jnp.where(hit, col, 0.0), axis=0, keepdims=True)

    def pcopy(e):
        return pltpu.make_async_remote_copy(
            src_ref=psend, dst_ref=precv.at[e],
            send_sem=ps_sem.at[0], recv_sem=pr_sem.at[0],
            device_id=peer(e), device_id_type=MESH)

    each(n - 1, lambda e: pcopy(e).start())
    for l in range(nl):
        each(ns - 1, lambda d: gcopy(l, d).wait_send())
        each(nr - 1, lambda d: tcopy(l, d).wait_send())

    pltpu.make_async_copy(precv, precv, pr_sem.at[0]).wait()
    picked_ref[...] = psend[...] + jnp.sum(precv[...], axis=0)
    pltpu.make_async_copy(precv, precv, ps_sem.at[0]).wait()


def body(nr, ns, activations, out_grads, lengths, proj_in, proj_out,
         basis_in, basis_out, eigen, store, candidates):
    nl, _, tok, width = activations.shape
    rank = proj_in.shape[2]
    rdev, flat = store.shape
    batch, topk = candidates.shape
    n = nr * ns
    dma = pltpu.SemaphoreType.DMA
    vm = pltpu.VMEM
    hbm = pl.BlockSpec(memory_space=pltpu.HBM)
    scores, picked = pl.pallas_call(
        functools.partial(kernel, nr, ns),
        out_shape=(pltpu.VMEM((batch, rdev), F32), pltpu.VMEM((batch, topk), F32)),
        in_specs=[pl.BlockSpec(memory_space=pltpu.SMEM)] + [hbm] * 9,
        out_specs=(pl.BlockSpec(memory_space=pltpu.VMEM),) * 2,
        scratch_shapes=[
            vm((nl, tok, width), BF16), vm((nl, tok, width), BF16),
            vm((nl, rank, width), BF16), vm((nl, rank, width), BF16),
            vm((nl, rank, rank), F32), vm((nl, rank, rank), F32), vm((nl, rank, rank), F32),
            vm((rdev, flat), BF16), vm((batch, topk), jnp.int32),
            vm((nl, rank // 2, 2 * rank), BF16), vm((nl, ns - 1, rank // 2, 2 * rank), BF16),
            vm((nl * rank // 2, 2 * rank), BF16), vm((nr - 1, nl * rank // 2, 2 * rank), BF16),
            vm((batch, topk), F32), vm((n - 1, batch, topk), F32),
            dma((nl, 4)), dma((5,)),
            dma((nl, ns - 1)), dma((nl, ns - 1)),
            dma((nl, nr - 1)), dma((nl, nr - 1)),
            dma((1,)), dma((1,)),
        ],
        compiler_params=pltpu.CompilerParams(
            collective_id=0, has_side_effects=True, vmem_limit_bytes=60 * 2**20),
    )(
        lengths, activations, out_grads,
        jnp.swapaxes(proj_in, 1, 2), jnp.swapaxes(proj_out, 1, 2),
        basis_in, basis_out, eigen, store, candidates,
    )
    return scores.T, picked


def solution(mesh):
    placed = (
        P(None, ("groups", "rows"), "seq", None),
        P(None, ("groups", "rows"), "seq", None),
        P(("groups", "rows")),
        P(),
        P(),
        P(),
        P(),
        P(),
        P(("groups", "rows", "seq"), None),
        P("groups", None),
    )
    return jax.shard_map(
        functools.partial(body, mesh.shape["rows"], mesh.shape["seq"]),
        mesh=mesh,
        in_specs=placed,
        out_specs=(P(("groups", "rows", "seq"), None), P("groups", None)),
        check_vma=False,
    )
```

```python
import functools

import jax
import jax.numpy as jnp
from jax import lax
from jax.experimental import pallas as pl
from jax.experimental.pallas import tpu as pltpu
from jax.sharding import PartitionSpec as P

damping = 1.0
MESH = pl.DeviceIdType.MESH
F32 = jnp.float32
BF16 = jnp.bfloat16
NN = (((1,), (0,)), ((), ()))
NT = (((1,), (1,)), ((), ()))


def mm(a, b, dims=NN):
    return lax.dot_general(a, b, dims, preferred_element_type=F32)


def split(x):
    hi = x.astype(BF16)
    return hi, (x - hi.astype(F32)).astype(BF16)


def mm3(a, b, dims=NN):
    return mm(a[0], b[0], dims) + (mm(a[0], b[1], dims) + mm(a[1], b[0], dims))


def project(weights, rows, l):
    quarter = rows.shape[2] // 4
    a, b, c, d = (
        mm(weights[l, :, i * quarter:(i + 1) * quarter], rows[l, :, i * quarter:(i + 1) * quarter], NT)
        for i in range(4))
    return (a + b) + (c + d)


def each(count, step):
    if count <= 16:
        for i in range(count):
            step(i)
    else:
        lax.fori_loop(0, count, lambda i, c: (step(i), c)[1], 0)


def kernel(
    nr, ns, lengths,
    acts_hbm, grads_hbm, pin_hbm, pout_hbm, bin_hbm, bout_hbm, eig_hbm, store_hbm, cand_hbm,
    scores_ref, picked_ref,
    acts, grads, pin, pout, bin_, bout, eig, store, cand,
    gsend, grecv, tsend, trecv, psend, precv,
    load_sem, small_sem, gs_sem, gr_sem, ts_sem, tr_sem, ps_sem, pr_sem,
):
    nl, tok, width = acts.shape
    rank = pin.shape[1]
    rdev = store.shape[0]
    half = rank // 2
    n = nr * ns
    row, seq = lax.axis_index("rows"), lax.axis_index("seq")
    me = row * ns + seq

    loads = []
    for l in range(nl):
        loads.append([
            pltpu.make_async_copy(src, dst, load_sem.at[l, i])
            for i, (src, dst) in enumerate((
                (pin_hbm.at[l], pin.at[l]),
                (acts_hbm.at[l, 0], acts.at[l]),
                (pout_hbm.at[l], pout.at[l]),
                (grads_hbm.at[l, 0], grads.at[l]),
            ))
        ])
    small = [
        pltpu.make_async_copy(src, dst, small_sem.at[i])
        for i, (src, dst) in enumerate((
            (bin_hbm, bin_), (bout_hbm, bout), (eig_hbm, eig), (cand_hbm, cand), (store_hbm, store),
        ))
    ]
    barrier = pltpu.get_barrier_semaphore()

    each(ns - 1, lambda d: pl.semaphore_signal(
        barrier, inc=1, device_id={"seq": lax.rem(seq + d + 1, ns)}, device_id_type=MESH))
    each(nr - 1, lambda d: pl.semaphore_signal(
        barrier, inc=1, device_id={"rows": lax.rem(row + d + 1, nr)}, device_id_type=MESH))

    for c in small[:4]:
        c.start()
    for group in loads:
        for c in group:
            c.start()
    small[4].start()

    def peer(e):
        to = lax.rem(me + e + 1, n)
        return {"rows": to // ns, "seq": lax.rem(to, ns)}

    for c in small[:3]:
        c.wait()
    i0 = lax.broadcasted_iota(jnp.int32, (rank, rank), 0)
    i1 = lax.broadcasted_iota(jnp.int32, (rank, rank), 1)
    order = (i1 == jnp.where(i0 < half, 2 * i0, 2 * (i0 - half) + 1)).astype(BF16)
    bi, bi2, bot, beo = [], [], [], []
    for l in range(nl):
        b = split(bin_[l])
        bi.append(b)
        bi2.append(tuple(jnp.concatenate([x, x], axis=0) for x in b))
        bot.append(split(jnp.transpose(bout[l])))
        beo.append(tuple(mm(order, x).astype(BF16) for x in split(bout[l])))

    pos = seq * tok + lax.broadcasted_iota(jnp.int32, (rank, tok), 1)
    keep = pos < lengths[0]

    def gcopy(l, d):
        return pltpu.make_async_remote_copy(
            src_ref=gsend.at[l], dst_ref=grecv.at[l, d],
            send_sem=gs_sem.at[l], recv_sem=gr_sem.at[l],
            device_id={"seq": lax.rem(seq + d + 1, ns)}, device_id_type=MESH)

    low = lax.broadcasted_iota(jnp.int32, (half, 2 * rank), 1) < rank
    own = []
    for l in range(nl):
        loads[l][0].wait()
        loads[l][1].wait()
        pat = jnp.where(keep, project(pin, acts, l), 0.0).astype(BF16)
        loads[l][2].wait()
        loads[l][3].wait()
        pgt = project(pout, grads, l).astype(BF16)
        g = mm(pgt, jnp.concatenate([pat, pat], axis=0), NT)
        g = jnp.where(low, g[:half], g[half:])
        own.append(g)
        gsend[l] = g.astype(BF16)
        if l == 0:
            pl.semaphore_wait(barrier, ns + nr - 2)
        each(ns - 1, lambda d: gcopy(l, d).start())

    def tcopy(l, d):
        part = pl.ds(l * half, half)
        return pltpu.make_async_remote_copy(
            src_ref=tsend.at[part], dst_ref=trecv.at[d, part],
            send_sem=ts_sem.at[l, d], recv_sem=tr_sem.at[l, d],
            device_id={"rows": lax.rem(row + d + 1, nr)}, device_id_type=MESH)

    for l in range(nl):
        total = own[l]
        pltpu.make_async_copy(grecv.at[l], grecv.at[l], gr_sem.at[l]).wait()
        total = total + jnp.sum(grecv[l].astype(F32), axis=0)
        total = jnp.concatenate([total[:, :rank], total[:, rank:]], axis=0)
        y = mm3(split(total), bi[l])
        rot = mm3(bot[l], split(y))
        pre = rot / (eig[l] + damping)
        x2 = mm3(split(pre), bi2[l], NT)
        z = mm3(beo[l], split(x2))
        t = jnp.where(low, z[:half], z[half:]).astype(BF16)
        tsend[pl.ds(l * half, half), :] = t
        each(nr - 1, lambda d: tcopy(l, d).start())

    for c in small[3:]:
        c.wait()
    lanes = 2 * rank
    eye = lax.broadcasted_iota(jnp.int32, (rdev, rdev), 0) == lax.broadcasted_iota(
        jnp.int32, (rdev, rdev), 1)
    rows_k = me * rdev + lax.broadcasted_iota(jnp.int32, (rdev, cand.shape[1]), 0)

    def partial(t, l):
        t = t.astype(F32)
        acc = [jnp.zeros((rdev, lanes), F32) for _ in range(2)]
        for c in range(half):
            at = (l * half + c) * lanes
            s = store[:, at:at + lanes].astype(F32)
            acc[c % 2] = acc[c % 2] + s * t[c:c + 1, :]
        return acc[0] + acc[1]

    sums = [None] * nr
    for l in range(nl):
        part = pl.ds(l * half, half)
        for p in range(nr):
            if p > 0:
                tcopy(l, p - 1).wait_recv()
            a = partial(tsend[part, :] if p == 0 else trecv[p - 1, part, :], l)
            sums[p] = a if l == 0 else sums[p] + a
            if l == nl - 1:
                b = lax.rem(row + nr - p, nr)
                col = jnp.sum(sums[p], axis=1, keepdims=True)
                scores_ref[pl.ds(b, 1), :] = jnp.sum(
                    jnp.where(eye, col, 0.0), axis=0, keepdims=True)
                hit = cand[pl.ds(b, 1), :] == rows_k
                psend[pl.ds(b, 1), :] = jnp.sum(
                    jnp.where(hit, col, 0.0), axis=0, keepdims=True)

    def pcopy(e):
        return pltpu.make_async_remote_copy(
            src_ref=psend, dst_ref=precv.at[e],
            send_sem=ps_sem.at[0], recv_sem=pr_sem.at[0],
            device_id=peer(e), device_id_type=MESH)

    each(n - 1, lambda e: pcopy(e).start())
    for l in range(nl):
        pltpu.make_async_copy(grecv.at[l], grecv.at[l], gs_sem.at[l]).wait()
        each(nr - 1, lambda d: tcopy(l, d).wait_send())

    pltpu.make_async_copy(precv, precv, pr_sem.at[0]).wait()
    picked_ref[...] = psend[...] + jnp.sum(precv[...], axis=0)
    pltpu.make_async_copy(precv, precv, ps_sem.at[0]).wait()


def body(nr, ns, activations, out_grads, lengths, proj_in, proj_out,
         basis_in, basis_out, eigen, store, candidates):
    nl, _, tok, width = activations.shape
    rank = proj_in.shape[2]
    rdev, flat = store.shape
    batch, topk = candidates.shape
    n = nr * ns
    dma = pltpu.SemaphoreType.DMA
    vm = pltpu.VMEM
    hbm = pl.BlockSpec(memory_space=pltpu.HBM)
    scores, picked = pl.pallas_call(
        functools.partial(kernel, nr, ns),
        out_shape=(pltpu.VMEM((batch, rdev), F32), pltpu.VMEM((batch, topk), F32)),
        in_specs=[pl.BlockSpec(memory_space=pltpu.SMEM)] + [hbm] * 9,
        out_specs=(pl.BlockSpec(memory_space=pltpu.VMEM),) * 2,
        scratch_shapes=[
            vm((nl, tok, width), BF16), vm((nl, tok, width), BF16),
            vm((nl, rank, width), BF16), vm((nl, rank, width), BF16),
            vm((nl, rank, rank), F32), vm((nl, rank, rank), F32), vm((nl, rank, rank), F32),
            vm((rdev, flat), BF16), vm((batch, topk), jnp.int32),
            vm((nl, rank // 2, 2 * rank), BF16), vm((nl, ns - 1, rank // 2, 2 * rank), BF16),
            vm((nl * rank // 2, 2 * rank), BF16), vm((nr - 1, nl * rank // 2, 2 * rank), BF16),
            vm((batch, topk), F32), vm((n - 1, batch, topk), F32),
            dma((nl, 4)), dma((5,)),
            dma((nl,)), dma((nl,)),
            dma((nl, nr - 1)), dma((nl, nr - 1)),
            dma((1,)), dma((1,)),
        ],
        compiler_params=pltpu.CompilerParams(
            collective_id=0, has_side_effects=True, vmem_limit_bytes=60 * 2**20),
    )(
        lengths, activations, out_grads,
        jnp.swapaxes(proj_in, 1, 2), jnp.swapaxes(proj_out, 1, 2),
        basis_in, basis_out, eigen, store, candidates,
    )
    return scores.T, picked


def solution(mesh):
    placed = (
        P(None, ("groups", "rows"), "seq", None),
        P(None, ("groups", "rows"), "seq", None),
        P(("groups", "rows")),
        P(),
        P(),
        P(),
        P(),
        P(),
        P(("groups", "rows", "seq"), None),
        P("groups", None),
    )
    return jax.shard_map(
        functools.partial(body, mesh.shape["rows"], mesh.shape["seq"]),
        mesh=mesh,
        in_specs=placed,
        out_specs=(P(("groups", "rows", "seq"), None), P("groups", None)),
        check_vma=False,
    )
```
